32 devices in a mesh: seq: 8 (over z, y), head: 4 (over x, core).
Axes of the slice: x: 2, y: 2, z: 4, core: 2. Of those that a mesh axis runs over, the one named last changes fastest.
Arguments:
- queries: bfloat16 [2048, 1024], P('seq', 'head'), may hold values from -8 to 8
- key_rows: bfloat16 [2048, 1024], P('seq', 'head'), may hold values from -8 to 8
- value_rows: bfloat16 [2048, 1024], P('seq', 'head'), may hold values from -6 to 6
- attn_out_grad: bfloat16 [2048, 1024], P('seq', 'head'), may hold values from -6 to 6
- ssm_input: bfloat16 [2048, 512], P('seq', 'head'), may hold values from -6 to 6
- b_matrix: bfloat16 [2048, 256], P('seq'), may hold values from -2 to 2
- c_matrix: bfloat16 [2048, 256], P('seq'), may hold values from -2 to 2
- step_sizes: float32 [2048, 8], P('seq', 'head'), may hold values from 0.005 to 0.05
- decay_rates: float32 [8], P('head'), may hold values from 0.00024414062 to 0.5
- skip_gain: float32 [8], P('head'), may hold values from 0.5 to 1.5
- ssm_out_grad: bfloat16 [2048, 512], P('seq', 'head'), may hold values from -6 to 6
- doc_lengths: int32 [8], replicated, may hold values from 1 to 512, 2048 in all
Outputs:
- attn_out: bfloat16 [2048, 1024], P('seq', 'head')
- query_grad: bfloat16 [2048, 1024], P('seq', 'head')
- key_grad: bfloat16 [2048, 1024], P('seq', 'head')
- value_grad: bfloat16 [2048, 1024], P('seq', 'head')
- ssm_out: bfloat16 [2048, 512], P('seq', 'head')
- input_grad: bfloat16 [2048, 512], P('seq', 'head')
- b_grad: float32 [2048, 256], P('seq')
- c_grad: float32 [2048, 256], P('seq')
The draws below stay inside these ranges and needn't reach their ends.
All inputs are finite; a program needn't handle non-finite values.
Results may differ from the reference program's by a relative error of at most 0.022.
Values may be sent and summed in bfloat16 or wider, within the bound.
No kernel may reach another device: no remote copies, remote signals or barrier semaphores. Data moves between devices by JAX's collectives and lax.ppermute only.
A program may use at most 128 MiB of HBM per device.

```python
import math
import jax
import jax.numpy as jnp
import numpy as np
from jax import lax

HEAD_DIM = 128
SSM_DIM = 64
STATE = 256
TOK_DEV = 256
MOST_DOC = 512
ATT_HEADS = 8
SSM_HEADS = 8
REACH = 2
SEQ_LEN = 2048
DOCS = 8
N_SEQ = 8


def paired_rows(key):
    paired_key = jax.random.fold_in(key, 4111)
    draw_one, draw_two = jax.random.split(paired_key, 2)
    array_shape = (SEQ_LEN, ATT_HEADS * HEAD_DIM)
    query_part = jax.random.normal(draw_one, array_shape, jnp.float32)
    key_part = jax.random.normal(draw_two, array_shape, jnp.float32)
    return (jnp.clip(query_part, -8.0, 8.0), jnp.clip(key_part, -8.0, 8.0))


def draw_queries(key, part):
    return paired_rows(key)[0].astype(jnp.bfloat16)


def draw_key_rows(key, part):
    return paired_rows(key)[1].astype(jnp.bfloat16)


def level_of(key, shape, cuts, smallest, high):
    loudness, own = 1.0, jax.random.fold_in(key, 6)
    for axis_at, blocks in cuts:
        steps = jnp.exp(jax.random.uniform(jax.random.fold_in(own, axis_at), (blocks,), jnp.float32, smallest / len(cuts), high / len(cuts)))
        loudness = loudness * jnp.repeat(steps, shape[axis_at] // blocks).reshape([-1 if axis == axis_at else 1 for axis in range(len(shape))])
    return loudness


def profile(count, total, reach, slope):
    portions = [(1 << 20) // math.isqrt(grade ** slope) + 1 for grade in range(2, count + 1)]
    surplus, given = total - reach - (count - 1), [1] * (count - 1)
    while surplus > 0:
        free = [i for i in range(count - 1) if given[i] < reach]
        mass, left = sum([portions[i] for i in free]), surplus
        for i in free:
            more = min(reach - given[i], max(1, left * portions[i] // mass), surplus)
            given[i] = given[i] + more
            surplus = surplus - more
    return np.array([reach] + given)


def ragged(stream_key, number_of, total, most, lean):
    if number_of == 2:
        one = jax.random.randint(stream_key, (), max(1, total - most), min(most, total - 1) + 1)
        return jnp.stack([one, total - one])
    tallies = jnp.asarray(profile(number_of, total, most, lean), jnp.int32)
    twos = (number_of - 1) // 2
    source_of, taker = tallies[1:1 + 2 * twos:2], tallies[2:2 + 2 * twos:2]
    margin = jnp.minimum(source_of - 1, most - taker)
    shifted = jax.random.randint(jax.random.fold_in(stream_key, 1), (twos,), 0, 1 << 20) % (margin + 1)
    tallies = tallies.at[1:1 + 2 * twos:2].set(source_of - shifted).at[2:2 + 2 * twos:2].set(taker + shifted)
    return tallies[jax.random.permutation(jax.random.fold_in(stream_key, 2), number_of)]


def normal_values(own_key, shape, spread, bound, pieces=(), kind=jnp.bfloat16):
    result = jax.random.normal(own_key, shape, jnp.float32) * spread
    if len(pieces) > 0:
        result = level_of(own_key, shape, pieces, -0.22, 0.18) * result
    return jnp.clip(result, min=-bound, max=bound).astype(kind)


def setup_inputs(seed: int = 0) -> dict:
    streams_of = jax.random.split(jax.random.key(seed), 13)
    queries = draw_queries(jax.random.fold_in(streams_of[12], 71), 0)
    key_rows = draw_key_rows(jax.random.fold_in(streams_of[12], 71), 0)
    value_rows = normal_values(streams_of[2], (SEQ_LEN, ATT_HEADS * HEAD_DIM), 1.0, 6.0, ((0, 8), (1, 4)))
    attn_out_grad = normal_values(streams_of[3], (SEQ_LEN, ATT_HEADS * HEAD_DIM), 1.0, 6.0, ((0, 8), (1, 4)))
    ssm_input = normal_values(streams_of[4], (SEQ_LEN, SSM_HEADS * SSM_DIM), 1.0, 6.0, ((0, 8), (1, 4)))
    b_matrix = normal_values(streams_of[5], (SEQ_LEN, STATE), 0.25, 2.0, ((0, 8),))
    c_matrix = normal_values(streams_of[6], (SEQ_LEN, STATE), 0.25, 2.0, ((0, 8),))
    step_sizes = jnp.clip(jnp.exp(math.log(0.05) - 2.3025851 * jax.random.uniform(streams_of[7], (SEQ_LEN, SSM_HEADS), jnp.float32) ** level_of(streams_of[7], (SEQ_LEN, SSM_HEADS), ((0, 8), (1, 4)), -0.2, 0.2)), 0.005, 0.05)
    decay_rates = jnp.clip(jnp.exp(math.log(0.5) - 7.624619 * jax.random.uniform(streams_of[8], (SSM_HEADS,), jnp.float32) ** level_of(streams_of[8], (SSM_HEADS,), ((0, 4),), -0.2, 0.2)), 0.00024414062, 0.5)
    skip_gain = jnp.clip(1.0 + 0.1 * jax.random.normal(streams_of[9], (SSM_HEADS,), jnp.float32), 0.5, 1.5)
    ssm_out_grad = normal_values(streams_of[10], (SEQ_LEN, SSM_HEADS * SSM_DIM), 1.0, 6.0, ((0, 8), (1, 4)))
    doc_lengths = ragged(streams_of[11], DOCS, SEQ_LEN, MOST_DOC, 2).astype(jnp.int32)
    return {"queries": queries, "key_rows": key_rows, "value_rows": value_rows, "attn_out_grad": attn_out_grad, "ssm_input": ssm_input, "b_matrix": b_matrix, "c_matrix": c_matrix, "step_sizes": step_sizes, "decay_rates": decay_rates, "skip_gain": skip_gain, "ssm_out_grad": ssm_out_grad, "doc_lengths": doc_lengths}


def doc_index(positions, doc_ends):
    return lax.optimization_barrier(jnp.sum((positions[:, None] >= doc_ends[None, :]).astype(jnp.int32), axis=1))

def visible_mask(query_pos, key_pos, doc_ends):
    same_doc = doc_index(query_pos, doc_ends)[:, None] == doc_index(key_pos, doc_ends)[None, :]
    return same_doc & (key_pos[None, :] <= query_pos[:, None]) & (key_pos[None, :] >= 0)

def attention(queries, key_rows, value_rows, attn_out_grad, doc_ends):
    columns = queries.shape[1]
    head_count = columns // HEAD_DIM
    window_rows = (REACH + 1) * TOK_DEV
    scale = HEAD_DIM ** (-0.5)
    front_pad = jnp.zeros((REACH * TOK_DEV, columns), queries.dtype)
    key_pad = jnp.concatenate([front_pad, key_rows], axis=0)
    value_pad = jnp.concatenate([front_pad, value_rows], axis=0)
    acc_pad = jnp.zeros(((N_SEQ + REACH) * TOK_DEV, columns), jnp.float32)

    def scan_step(running, block_index):
        key_acc, value_acc = running
        row_start = (block_index * TOK_DEV).astype(jnp.int32)
        query_block = lax.dynamic_slice_in_dim(queries, row_start, TOK_DEV, 0).reshape(TOK_DEV, head_count, HEAD_DIM).astype(jnp.float32)
        grad_block = lax.dynamic_slice_in_dim(attn_out_grad, row_start, TOK_DEV, 0).reshape(TOK_DEV, head_count, HEAD_DIM).astype(jnp.float32)
        key_block = lax.dynamic_slice_in_dim(key_pad, row_start, window_rows, 0).reshape(window_rows, head_count, HEAD_DIM).astype(jnp.float32)
        value_block = lax.dynamic_slice_in_dim(value_pad, row_start, window_rows, 0).reshape(window_rows, head_count, HEAD_DIM).astype(jnp.float32)
        query_pos = row_start + jnp.arange(TOK_DEV, dtype=jnp.int32)
        key_pos = row_start - REACH * TOK_DEV + jnp.arange(window_rows, dtype=jnp.int32)
        tile_mask = visible_mask(query_pos, key_pos, doc_ends)[None]
        scores = jnp.einsum('thd,shd->hts', query_block, key_block) * scale
        scores = jnp.where(tile_mask, scores, -jnp.inf)
        row_top = lax.optimization_barrier(jnp.max(scores, axis=-1, keepdims=True))
        row_total = lax.optimization_barrier(jnp.sum(jnp.exp(scores - row_top), axis=-1, keepdims=True))
        tile_probs = jnp.where(tile_mask, jnp.exp(scores - row_top) / row_total, 0.0)
        probs_low = lax.optimization_barrier(tile_probs.astype(jnp.bfloat16)).astype(jnp.float32)
        attn_block = jnp.einsum('hts,shd->thd', probs_low, value_block).astype(jnp.bfloat16)
        row_delta = jnp.einsum('thd,thd->ht', grad_block, attn_block.astype(jnp.float32))
        prob_grad = jnp.einsum('thd,shd->hts', grad_block, value_block)
        dscore = (tile_probs * (prob_grad - row_delta[:, :, None]) * scale).astype(jnp.bfloat16)
        dscore = lax.optimization_barrier(dscore).astype(jnp.float32)
        query_part = jnp.einsum('hts,shd->thd', dscore, key_block).astype(jnp.bfloat16)
        key_part = jnp.einsum('hts,thd->shd', dscore, query_block).reshape(window_rows, columns)
        value_part = jnp.einsum('hts,thd->shd', probs_low, grad_block).reshape(window_rows, columns)
        key_acc = lax.dynamic_update_slice_in_dim(key_acc, lax.dynamic_slice_in_dim(key_acc, row_start, window_rows, 0) + key_part, row_start, 0)
        value_acc = lax.dynamic_update_slice_in_dim(value_acc, lax.dynamic_slice_in_dim(value_acc, row_start, window_rows, 0) + value_part, row_start, 0)
        return ((key_acc, value_acc), (attn_block.reshape(TOK_DEV, columns), query_part.reshape(TOK_DEV, columns)))
    (key_acc, value_acc), (attn_blocks, query_blocks) = lax.scan(scan_step, (acc_pad, acc_pad), jnp.arange(N_SEQ, dtype=jnp.int32))
    attn_out = attn_blocks.reshape(N_SEQ * TOK_DEV, columns)
    query_grad = query_blocks.reshape(N_SEQ * TOK_DEV, columns)
    key_grad = key_acc[REACH * TOK_DEV:].astype(jnp.bfloat16)
    value_grad = value_acc[REACH * TOK_DEV:].astype(jnp.bfloat16)
    return (attn_out, query_grad, key_grad, value_grad)

def ssm_parts(x_heads, b_rows, c_rows, step_sizes, decay_rates, skip_gain):
    row_count = x_heads.shape[0]
    offsets = jnp.arange(row_count, dtype=jnp.int32)
    log_decay = jnp.cumsum(-step_sizes * decay_rates[None, :], axis=0)
    causal = offsets[None, :] <= offsets[:, None]
    log_gaps = log_decay.T[:, :, None] - log_decay.T[:, None, :]
    fading = jnp.where(causal[None], jnp.exp(jnp.where(causal[None], log_gaps, 0.0)), 0.0)
    intersection = jnp.dot(c_rows, b_rows.T, precision=lax.Precision.HIGHEST)
    mixing = intersection[None] * fading * step_sizes.T[:, None, :]
    direct = jnp.einsum('hts,shp->thp', mixing, x_heads, precision=lax.Precision.HIGHEST)
    direct = direct + skip_gain[None, :, None] * x_heads
    carry_weight = jnp.exp(log_decay)
    tail_weight = jnp.exp(log_decay[-1][None, :] - log_decay) * step_sizes
    local_state = jnp.einsum('th,tn,thp->hnp', tail_weight, b_rows, x_heads, precision=lax.Precision.HIGHEST)
    decay_all = jnp.exp(log_decay[-1])
    return (direct, local_state, decay_all, carry_weight)

def ssm_forward(x_all, b_all, c_all, step_sizes, decay_rates, skip_gain):
    head_count = decay_rates.shape[0]
    x_blocks = x_all.reshape(N_SEQ, TOK_DEV, head_count, -1)
    b_blocks = b_all.reshape(N_SEQ, TOK_DEV, -1)
    c_blocks = c_all.reshape(N_SEQ, TOK_DEV, -1)
    step_blocks = step_sizes.reshape(N_SEQ, TOK_DEV, head_count)

    def scan_step(carry_state, block_items):
        x_heads, b_rows, c_rows, step_block = block_items
        direct, local_state, decay_all, carry_weight = ssm_parts(x_heads, b_rows, c_rows, step_block, decay_rates, skip_gain)
        incoming = jnp.einsum('tn,hnp->thp', c_rows, carry_state, precision=lax.Precision.HIGHEST)
        ssm_rows = direct + carry_weight[:, :, None] * incoming
        return (decay_all[:, None, None] * carry_state + local_state, ssm_rows)
    state_zero = jnp.zeros((head_count, b_all.shape[1], x_blocks.shape[-1]), x_all.dtype)
    items = (x_blocks, b_blocks, c_blocks, step_blocks)
    _, ssm_blocks = lax.scan(jax.checkpoint(scan_step), state_zero, items)
    return ssm_blocks.reshape(x_all.shape)

def reference(queries, key_rows, value_rows, attn_out_grad, ssm_input, b_matrix, c_matrix, step_sizes, decay_rates, skip_gain, ssm_out_grad, doc_lengths):
    doc_ends = jnp.cumsum(doc_lengths, dtype=jnp.int32)
    attn_out, query_grad, key_grad, value_grad = attention(queries, key_rows, value_rows, attn_out_grad, doc_ends)

    def forward(x_value, b_value, c_value):
        return ssm_forward(x_value, b_value, c_value, step_sizes, decay_rates, skip_gain)
    ssm_rows, pullback = jax.vjp(forward, ssm_input.astype(jnp.float32), b_matrix.astype(jnp.float32), c_matrix.astype(jnp.float32))
    x_grad, b_grad, c_grad = pullback(ssm_out_grad.astype(jnp.float32))
    return (attn_out, query_grad, key_grad, value_grad, ssm_rows.astype(jnp.bfloat16), x_grad.astype(jnp.bfloat16), b_grad, c_grad)
```

```python
import functools
import math

import jax
import jax.numpy as jnp
from jax import lax
from jax.experimental import pallas as pl
from jax.experimental.pallas import tpu as pltpu
from jax.sharding import PartitionSpec as P

HEAD_DIM = 128
REACH = 2
F32 = jnp.float32
BF16 = jnp.bfloat16
SCALE = HEAD_DIM ** (-0.5)
SCALE_LOG2E = SCALE * math.log2(math.e)
HIDDEN = -1e30

VMEM = pl.BlockSpec(memory_space=pltpu.VMEM)
SMEM = pl.BlockSpec(memory_space=pltpu.SMEM)


def mm(a, b):
    return lax.dot_general(a, b, (((1,), (0,)), ((), ())), preferred_element_type=F32)


def mm_nt(a, b):
    return lax.dot_general(a, b, (((1,), (1,)), ((), ())), preferred_element_type=F32)


def mm_tn(a, b):
    return lax.dot_general(a, b, (((0,), (0,)), ((), ())), preferred_element_type=F32)


def call(kernel, outs, in_specs, name, flops, *args, scratch=()):
    moved = sum(a.size * a.dtype.itemsize for a in args)
    moved += sum(math.prod(s) * jnp.dtype(d).itemsize for s, d in outs)
    return pl.pallas_call(
        kernel,
        out_shape=[jax.ShapeDtypeStruct(s, d) for s, d in outs],
        in_specs=in_specs,
        out_specs=[VMEM] * len(outs),
        scratch_shapes=list(scratch),
        name=name,
        cost_estimate=pl.CostEstimate(flops=flops, bytes_accessed=moved, transcendentals=0),
    )(*args)


def shifted(x, axis, by):
    length = lax.axis_size(axis)
    return lax.ppermute(x, axis, [(i, i + by) for i in range(length) if 0 <= i + by < length])


def swapped(x, axis, bit):
    return lax.ppermute(x, axis, [(i, i ^ bit) for i in range(lax.axis_size(axis))])


def by_head(shape, width, values):
    lane = lax.broadcasted_iota(jnp.int32, shape, 1)
    full = jnp.broadcast_to(values[0], shape)
    for h in range(1, len(values)):
        full = jnp.where(lane >= h * width, jnp.broadcast_to(values[h], shape), full)
    return full


def first_kernel(
    rate, q, k, v, do, x, g, b, c, dt, kv, qg, uv, msg, ew
):
    rows, cols = x.shape
    heads = dt.shape[1]
    width = cols // heads
    kv[:rows, :] = k[...]
    kv[rows:, :] = v[...]
    qg[:rows, :] = q[...]
    qg[rows:, :] = do[...]
    dts = by_head((rows, cols), width, [dt[:, h : h + 1] for h in range(heads)])
    lane = lax.broadcasted_iota(jnp.int32, (1, cols), 1)
    rates = jnp.full((1, cols), rate[0], F32)
    for h in range(1, heads):
        rates = jnp.where(lane >= h * width, rate[h], rates)
    logs = dts * (-rates)
    tri = (
        lax.broadcasted_iota(jnp.int32, (rows, rows), 1)
        <= lax.broadcasted_iota(jnp.int32, (rows, rows), 0)
    ).astype(F32).astype(BF16)
    high = logs.astype(BF16)
    rest = logs - high.astype(F32)
    mid = rest.astype(BF16)
    low = (rest - mid.astype(F32)).astype(BF16)
    total = mm(tri, high) + mm(tri, mid) + mm(tri, low)
    grow = jnp.exp(total)
    weight = dts * jnp.exp(-total)
    ew[:rows, :] = grow
    ew[rows:, :] = weight
    u = (weight * x[...].astype(F32)).astype(BF16)
    w = (grow * g[...].astype(F32)).astype(BF16)
    uv[:rows, :] = u
    uv[rows:, :] = w
    n = b.shape[1]
    state = mm_tn(u, b[...])
    ahead = mm_tn(w, c[...])
    row = lax.broadcasted_iota(jnp.int32, (16, n), 0)
    ends = jnp.zeros((16, n), F32)
    for h in range(heads):
        end = jnp.sum(dt[:, h : h + 1], axis=0, keepdims=True) * (-rate[h])
        end = jnp.broadcast_to(end, (1, n))
        ends = jnp.where(row == h, jnp.broadcast_to(end, (16, n)), ends)
        sl = slice(h * width, (h + 1) * width)
        msg[sl, :] = (state[sl, :] * jnp.exp(end)).astype(BF16)
    msg[cols : 2 * cols, :] = ahead.astype(BF16)
    top = ends.astype(BF16)
    msg[2 * cols : 2 * cols + 16, :] = top
    msg[2 * cols + 16 :, :] = (ends - top.astype(F32)).astype(BF16)


def decay_of(msg, cols):
    return msg[2 * cols : 2 * cols + 16, :].astype(F32) + msg[2 * cols + 16 :, :].astype(F32)


def join_kernel(heads, bit, first, last, mine, other, *refs):
    if first:
        sent, kept = refs
    else:
        held, sent, kept = refs
    cols = (mine.shape[0] - 32) // 2
    width = cols // heads
    index = lax.axis_index("seq")
    upper = (index & bit) != 0
    log_mine, log_other = decay_of(mine, cols), decay_of(other, cols)
    fade_mine, fade_other = jnp.exp(log_mine), jnp.exp(log_other)
    if first:
        log_before = log_after = jnp.zeros_like(log_mine)
    else:
        log_before = held[2 * cols : 2 * cols + 16, :]
        log_after = held[2 * cols + 16 :, :]
    before, after = jnp.exp(log_before), jnp.exp(log_after)
    low_fade = jnp.where(upper, fade_other, fade_mine)
    high_fade = jnp.where(upper, fade_mine, fade_other)
    next_upper = (index & (2 * bit)) != 0
    for h in range(heads):
        sl = slice(h * width, (h + 1) * width)
        al = slice(cols + h * width, cols + (h + 1) * width)
        s_mine, s_other = mine[sl, :].astype(F32), other[sl, :].astype(F32)
        a_mine, a_other = mine[al, :].astype(F32), other[al, :].astype(F32)
        zero = jnp.zeros_like(s_mine)
        add_s = jnp.where(upper, before[h : h + 1, :] * s_other, zero)
        add_a = jnp.where(upper, zero, after[h : h + 1, :] * a_other)
        if first:
            kept[sl, :] = add_s
            kept[al, :] = add_a
        else:
            kept[sl, :] = held[sl, :] + add_s
            kept[al, :] = held[al, :] + add_a
        low_s, high_s = jnp.where(upper, s_other, s_mine), jnp.where(upper, s_mine, s_other)
        low_a, high_a = jnp.where(upper, a_other, a_mine), jnp.where(upper, a_mine, a_other)
        s_new = high_fade[h : h + 1, :] * low_s + high_s
        a_new = low_fade[h : h + 1, :] * high_a + low_a
        if last:
            sent[sl, :] = jnp.where(next_upper, a_new, s_new).astype(BF16)
        else:
            sent[sl, :] = s_new.astype(BF16)
            sent[al, :] = a_new.astype(BF16)
    kept[2 * cols : 2 * cols + 16, :] = log_before + jnp.where(upper, log_other, 0.0)
    kept[2 * cols + 16 :, :] = log_after + jnp.where(upper, 0.0, log_other)
    if not last:
        log_new = log_mine + log_other
        top = log_new.astype(BF16)
        sent[2 * cols : 2 * cols + 16, :] = top
        sent[2 * cols + 16 :, :] = (log_new - top.astype(F32)).astype(BF16)


def entry_kernel(heads, bit, msg, held, other, st):
    cols = other.shape[0]
    width = cols // heads
    upper = (lax.axis_index("seq") & bit) != 0
    ends = jnp.exp(decay_of(msg, cols))
    before = jnp.exp(held[2 * cols : 2 * cols + 16, :])
    after = jnp.exp(held[2 * cols + 16 :, :])
    for h in range(heads):
        sl = slice(h * width, (h + 1) * width)
        al = slice(cols + h * width, cols + (h + 1) * width)
        far = other[sl, :].astype(F32)
        zero = jnp.zeros_like(far)
        s = held[sl, :] + jnp.where(upper, before[h : h + 1, :] * far, zero)
        a = held[al, :] + jnp.where(upper, zero, after[h : h + 1, :] * far)
        st[sl, :] = s.astype(BF16)
        st[al, :] = (a * ends[h : h + 1, :]).astype(BF16)


def ssm_kernel(masks, gain, *refs):
    count = len(masks)
    uv, st = refs[:count], refs[count : 2 * count]
    b, c, x, g, ew, y, xg, bg, cg, uv_all, st_all = refs[2 * count :]
    rows, cols = x.shape
    heads = gain.shape[0]
    lane = lax.broadcasted_iota(jnp.int32, (1, cols), 1)
    gains = jnp.full((1, cols), gain[0], F32)
    for h in range(1, heads):
        gains = jnp.where(lane >= h * (cols // heads), gain[h], gains)
    me = lax.axis_index("head")
    for j in range(count):
        uv_all[me ^ masks[j]] = uv[j][...]
        st_all[me ^ masks[j]] = st[j][...]
    across = lax.broadcasted_iota(jnp.int32, (rows, rows), 1)
    down = lax.broadcasted_iota(jnp.int32, (rows, rows), 0)
    causal, anti = across <= down, down <= across
    b_rows, c_rows = b[...], c[...]
    near = jnp.where(causal, mm_nt(c_rows, b_rows), 0.0).astype(BF16)
    near_t = jnp.where(anti, mm_nt(b_rows, c_rows), 0.0).astype(BF16)
    out = mm(near, uv[0][:rows, :]) + mm_nt(c_rows, st[0][:cols, :])
    y[...] = (ew[:rows, :] * out + gains * x[...].astype(F32)).astype(BF16)
    back = mm(near_t, uv[0][rows:, :]) + mm_nt(b_rows, st[0][cols:, :])
    xg[...] = (ew[rows:, :] * back + gains * g[...].astype(F32)).astype(BF16)
    slope = jnp.zeros((rows, rows), F32)
    slope_t = jnp.zeros((rows, rows), F32)
    b_sum = jnp.zeros(bg.shape, F32)
    c_sum = jnp.zeros(cg.shape, F32)
    for j in range(count):
        u, w = uv_all[j, :rows, :], uv_all[j, rows:, :]
        slope = slope + mm_nt(w, u)
        slope_t = slope_t + mm_nt(u, w)
        c_sum = c_sum + mm(w, st_all[j, :cols, :])
        b_sum = b_sum + mm(u, st_all[j, cols:, :])
    slope = jnp.where(causal, slope, 0.0).astype(BF16)
    slope_t = jnp.where(anti, slope_t, 0.0).astype(BF16)
    cg[...] = mm(slope, b_rows) + c_sum
    bg[...] = mm(slope_t, c_rows) + b_sum


def starts_of(lengths, pos):
    def lap(j, carry):
        start, at = carry
        return jnp.where(pos >= at, at, start), at + lengths[j]

    docs = lengths.shape[0]
    return lax.fori_loop(0, docs, lap, (jnp.zeros_like(pos), jnp.int32(0)), unroll=docs <= 8)[0]


def forward_kernel(lengths, qg, kv, kv1, kv2, out, dq, stats):
    rows = qg.shape[0] // 2
    base = lax.axis_index("seq") * rows
    pos = base + lax.broadcasted_iota(jnp.int32, (rows, HEAD_DIM), 0)
    start = starts_of(lengths, pos) - base
    start = jnp.concatenate([start] * (rows // HEAD_DIM), axis=1)
    key = lax.broadcasted_iota(jnp.int32, (rows, rows), 1)
    query = lax.broadcasted_iota(jnp.int32, (rows, rows), 0)
    masks = [(key >= start) & (key <= query)]
    masks += [key - d * rows >= start for d in (1, 2)]
    lane = lax.broadcasted_iota(jnp.int32, (rows, HEAD_DIM), 1)
    heads = qg.shape[1] // HEAD_DIM
    collected = jnp.zeros((rows, HEAD_DIM), F32)
    for h in range(heads):
        sl = slice(h * HEAD_DIM, (h + 1) * HEAD_DIM)
        qh, gh = qg[:rows, sl], qg[rows:, sl]
        keys = [r[:rows, sl] for r in (kv, kv1, kv2)]
        values = [r[rows:, sl] for r in (kv, kv1, kv2)]
        scores = [
            jnp.where(m, mm_nt(qh, kk) * SCALE_LOG2E, HIDDEN) for m, kk in zip(masks, keys)
        ]
        top = functools.reduce(jnp.maximum, scores)
        top = jnp.max(top, axis=1, keepdims=True)
        parts = [jnp.exp2(s - top) for s in scores]
        total = jnp.sum(functools.reduce(jnp.add, parts), axis=1, keepdims=True)
        inverse = 1.0 / total
        probs = [p * inverse for p in parts]
        low = [p.astype(BF16) for p in probs]
        rows_out = functools.reduce(jnp.add, [mm(p, vv) for p, vv in zip(low, values)])
        rows_out = rows_out.astype(BF16)
        out[:, sl] = rows_out
        delta = jnp.sum(gh.astype(F32) * rows_out.astype(F32), axis=1, keepdims=True)
        slopes = [
            (p * (mm_nt(gh, vv) - delta)).astype(BF16) for p, vv in zip(probs, values)
        ]
        grad = functools.reduce(jnp.add, [mm(s, kk) for s, kk in zip(slopes, keys)])
        dq[:, sl] = (grad * SCALE).astype(BF16)
        level = top + jnp.log2(total)
        collected = jnp.where(lane == h, level, collected)
        collected = jnp.where(lane == heads + h, delta, collected)
    stats[...] = jnp.transpose(collected)[: stats.shape[0], :]


def backward_kernel(lengths, kv, qg, qg1, qg2, s0, s1, s2, dk, dv):
    rows = kv.shape[0] // 2
    base = lax.axis_index("seq") * rows
    key = lax.broadcasted_iota(jnp.int32, (rows, rows), 0)
    query = lax.broadcasted_iota(jnp.int32, (rows, rows), 1)
    masks = []
    for d in range(REACH + 1):
        pos = base + d * rows + lax.broadcasted_iota(jnp.int32, (8, rows), 1)
        start = (starts_of(lengths, pos) - base)[:1, :]
        mask = key >= start
        masks.append(mask & (key <= query) if d == 0 else mask)
    heads = kv.shape[1] // HEAD_DIM
    for h in range(heads):
        sl = slice(h * HEAD_DIM, (h + 1) * HEAD_DIM)
        kh, vh = kv[:rows, sl], kv[rows:, sl]
        key_sum = value_sum = None
        for mask, far, st in zip(masks, (qg, qg1, qg2), (s0, s1, s2)):
            qh, gh = far[:rows, sl], far[rows:, sl]
            scores = jnp.where(mask, mm_nt(kh, qh) * SCALE_LOG2E - st[h : h + 1, :], HIDDEN)
            probs = jnp.exp2(scores)
            slope = probs * (mm_nt(vh, gh) - st[heads + h : heads + h + 1, :])
            key_part = mm(slope.astype(BF16), qh)
            value_part = mm(probs.astype(BF16), gh)
            key_sum = key_part if key_sum is None else key_sum + key_part
            value_sum = value_part if value_sum is None else value_sum + value_part
        dk[:, sl] = (key_sum * SCALE).astype(BF16)
        dv[:, sl] = value_sum.astype(BF16)


def on_device(
    queries,
    key_rows,
    value_rows,
    attn_out_grad,
    ssm_input,
    b_matrix,
    c_matrix,
    step_sizes,
    decay_rates,
    skip_gain,
    ssm_out_grad,
    doc_lengths,
):
    rows, att_cols = queries.shape
    cols = ssm_input.shape[1]
    n = b_matrix.shape[1]
    heads = step_sizes.shape[1]
    seq_size, head_size = lax.axis_size("seq"), lax.axis_size("head")
    kv, qg, uv, msg, ew = call(
        first_kernel,
        [
            ((2 * rows, att_cols), BF16),
            ((2 * rows, att_cols), BF16),
            ((2 * rows, cols), BF16),
            ((2 * cols + 32, n), BF16),
            ((2 * rows, cols), F32),
        ],
        [SMEM] + [VMEM] * 9,
        "first",
        10**8,
        decay_rates,
        queries,
        key_rows,
        value_rows,
        attn_out_grad,
        ssm_input,
        ssm_out_grad,
        b_matrix,
        c_matrix,
        step_sizes,
    )
    kv1, kv2 = shifted(kv, "seq", 1), shifted(kv, "seq", 2)
    qg1, qg2 = shifted(qg, "seq", -1), shifted(qg, "seq", -2)

    def spread(block):
        blocks, masks, bit = [block], [0], head_size // 2
        while bit:
            blocks = blocks + [swapped(one, "head", bit) for one in blocks]
            masks = masks + [m ^ bit for m in masks]
            bit //= 2
        return blocks, masks

    uvs, masks = spread(uv)
    held, sent, bit = None, msg, 1
    while 2 * bit < seq_size:
        last = 4 * bit >= seq_size
        other = swapped(sent, "seq", bit)
        first = held is None
        sent, held = call(
            functools.partial(join_kernel, heads, bit, first, last),
            [((cols if last else 2 * cols + 32, n), BF16), ((2 * cols + 32, n), F32)],
            [VMEM] * (2 if first else 3),
            f"join{bit}",
            10**6,
            *((sent, other) if first else (sent, other, held)),
        )
        bit *= 2
    other = swapped(sent, "seq", bit)
    (st,) = call(
        functools.partial(entry_kernel, heads, bit),
        [((2 * cols, n), BF16)],
        [VMEM] * 3,
        "entry",
        10**6,
        msg,
        held,
        other,
    )
    sts, _ = spread(st)
    attn_out, query_grad, s0 = call(
        forward_kernel,
        [((rows, att_cols), BF16), ((rows, att_cols), BF16), ((8, rows), F32)],
        [SMEM] + [VMEM] * 4,
        "forward",
        10**9,
        doc_lengths,
        qg,
        kv,
        kv1,
        kv2,
    )
    s1, s2 = shifted(s0, "seq", -1), shifted(s0, "seq", -2)
    key_grad, value_grad = call(
        backward_kernel,
        [((rows, att_cols), BF16), ((rows, att_cols), BF16)],
        [SMEM] + [VMEM] * 7,
        "backward",
        10**9,
        doc_lengths,
        kv,
        qg,
        qg1,
        qg2,
        s0,
        s1,
        s2,
    )
    ssm_out, input_grad, b_grad, c_grad = call(
        functools.partial(ssm_kernel, tuple(masks)),
        [((rows, cols), BF16), ((rows, cols), BF16), ((rows, n), F32), ((rows, n), F32)],
        [SMEM] + [VMEM] * (2 * head_size + 5),
        "ssm",
        10**9,
        skip_gain,
        *uvs,
        *sts,
        b_matrix,
        c_matrix,
        ssm_input,
        ssm_out_grad,
        ew,
        scratch=(
            pltpu.VMEM((head_size, 2 * rows, cols), BF16),
            pltpu.VMEM((head_size, 2 * cols, n), BF16),
        ),
    )
    return (attn_out, query_grad, key_grad, value_grad, ssm_out, input_grad, b_grad, c_grad)


def solution(mesh):
    wide, narrow = P("seq", "head"), P("seq", None)
    return jax.shard_map(
        on_device,
        mesh=mesh,
        in_specs=(wide,) * 5 + (narrow, narrow, wide, P("head"), P("head"), wide, P()),
        out_specs=(wide,) * 6 + (narrow, narrow),
        check_vma=False,
    )
```
